32 devices in a mesh: groups: 2 (over x), month: 16 (over z, y, core).
Axes of the slice: x: 2, y: 2, z: 4, core: 2. Of those that a mesh axis runs over, the one named last changes fastest.
Arguments:
- shocks: float32 [512, 4096], P('month', 'groups'), parts along dimension 1, may hold values from -6 to 6
- long_mean: float32 [512], P('month'), may hold values from 0 to 0.08
- reversion: float32 [4096], P('groups'), parts along dimension 0, may hold values from 0.1 to 1
- volatility: float32 [4096], P('groups'), parts along dimension 0, may hold values from 0.004 to 0.015
- start_rate: float32 [4096], P('groups'), parts along dimension 0, may hold values from 0 to 0.06
- cash_flows: bfloat16 [3, 512, 24576], P(None, 'month', 'groups'), parts along dimension 2, may hold values from -0.5 to 0.5
Outputs:
- present: bfloat16 [3, 24576, 2048], P(None, ('groups', 'month')), parts along dimension 1
The draws below stay inside these ranges and needn't reach their ends.
There are 2 independent parts, one for each index of `groups`. The reference program is written for one: setup_inputs(seed, part) draws one part's arguments, and reference() takes and returns one part's arrays. A program takes and returns all parts, laid end to end along the dimension named above; an argument that names none is the same for every part. Nothing has to cross between parts.
All inputs are finite; a program needn't handle non-finite values.
Results may differ from the reference program's by a relative error of at most 0.0049.
Values may be sent and summed in bfloat16 or wider, within the bound.
A program may use at most 192 MiB of HBM per device.

```python
import math
import jax
import jax.numpy as jnp
from jax import lax

LEGS = 3
MONTHS = 512
SCENARIOS = 2048
CELLS = 12288


def block_scale(own_key, dims, pieces, least, high):
    def one(dim, blocks):
        steps = jax.random.uniform(jax.random.fold_in(jax.random.fold_in(own_key, 6), dim), (blocks,), jnp.float32, least / len(pieces), high / len(pieces))
        return jnp.repeat(jnp.exp(steps), dims[dim] // blocks).reshape((-1,) + (1,) * (len(dims) - dim - 1))

    level = one(*pieces[0])
    for cut in pieces[1:]:
        level = level * one(*cut)
    return level


def gaussian(key, extent, deviation, bound, pieces=(), dtype=jnp.bfloat16):
    drawn = deviation * jax.random.normal(key, extent, jnp.float32)
    if pieces:
        drawn = drawn * block_scale(key, extent, pieces, -0.22, 0.18)
    return jnp.clip(drawn, -bound, bound).astype(dtype)


def setup_inputs(seed: int = 0, part: int = 0) -> dict:
    seeds = jax.random.split(jax.random.key(seed), 7)
    part_keys = jax.random.split(jax.random.fold_in(seeds[6], part), 7)
    shocks = gaussian(part_keys[0], (MONTHS, SCENARIOS), 1.0, 6.0, ((0, 16),), jnp.float32)
    long_mean = jnp.clip(0.08 * jax.random.uniform(seeds[1], (MONTHS,), jnp.float32) ** block_scale(seeds[1], (MONTHS,), ((0, 16),), -0.2, 0.2), 0.0, 0.08)
    reversion = jnp.clip(jnp.exp(jax.random.uniform(part_keys[2], (SCENARIOS,), jnp.float32, math.log(0.1), math.log(1.0))), 0.1, 1.0)
    volatility = jnp.clip(jnp.exp(jax.random.uniform(part_keys[3], (SCENARIOS,), jnp.float32, math.log(0.004), math.log(0.015))), 0.004, 0.015)
    start_rate = jnp.clip(jax.random.uniform(part_keys[4], (SCENARIOS,), jnp.float32, 0.0, 0.06), 0.0, 0.06)
    cash_flows = gaussian(part_keys[5], (LEGS, MONTHS, CELLS), (MONTHS // 4) ** -0.5, 0.5, ((1, 16),))
    return dict(shocks=shocks, long_mean=long_mean, reversion=reversion, volatility=volatility, start_rate=start_rate, cash_flows=cash_flows)


month_step = 1.0 / 12.0
root_step = math.sqrt(1.0 / 12.0)
risk_price = 0.15
price_scale = risk_price * math.sqrt(12.0)
price_drift = 0.5 * risk_price * risk_price

def reference(shocks, long_mean, reversion, volatility, start_rate, cash_flows):
    persist = 1.0 - reversion * month_step

    def advance(carry, inputs):
        rate, total = carry
        shock_row, level = inputs
        drive = reversion * month_step * level + volatility * root_step * shock_row
        rate = persist * rate + drive
        total = total + rate + price_scale * shock_row + price_drift
        return ((rate, total), jnp.exp(-month_step * total).astype(jnp.bfloat16))
    initial = (start_rate, jnp.zeros_like(start_rate))
    final_state, discount = lax.scan(advance, initial, (shocks, long_mean))
    blocks = []
    for leg_index in range(cash_flows.shape[0]):
        value = lax.dot_general(cash_flows[leg_index], discount, (((0,), (0,)), ((), ())), preferred_element_type=jnp.float32)
        blocks.append(value.astype(jnp.bfloat16))
    return jnp.stack(blocks)
```

```python
import functools
import math

import jax
import jax.numpy as jnp
from jax import lax
from jax.experimental import pallas as pl
from jax.experimental.pallas import tpu as pltpu
from jax.sharding import PartitionSpec as P

month_step = 1.0 / 12.0
root_step = math.sqrt(1.0 / 12.0)
risk_price = 0.15
price_scale = risk_price * math.sqrt(12.0)
price_drift = 0.5 * risk_price * risk_price
MESH = pl.DeviceIdType.MESH
CORES = 2


def kernel(
    n,
    sides,
    shocks,
    long_mean,
    reversion,
    volatility,
    start_rate,
    cash_flows,
    flows_out,
    discount_out,
    reach_ref,
    total_ref,
    part_ref,
    level_ref,
    block_ref,
    stage_ref,
    flow_send,
    flow_recv,
    part_send,
    part_recv,
    level_send,
    level_recv,
    up_send,
    up_recv,
    down_send,
    down_recv,
    side_send,
    side_recv,
    twin_send,
    twin_recv,
    own_sem,
):
    rows, width = shocks.shape
    legs = cash_flows.shape[0]
    own = cash_flows.shape[2] // n
    team = sides * CORES
    depth = n // team
    me = lax.axis_index("month")
    z, spot = me // team, me % team
    side, core = spot // CORES, spot % CORES
    place = lambda z, side, core: (z * sides + side) * CORES + core

    def remote(src, dst, send, recv, device):
        return pltpu.make_async_remote_copy(
            src_ref=src,
            dst_ref=dst,
            send_sem=send,
            recv_sem=recv,
            device_id={"month": device},
            device_id_type=MESH,
        )

    barrier = pltpu.get_barrier_semaphore()
    for k in range(1, n):
        pl.semaphore_signal(
            barrier, inc=1, device_id={"month": (me + k) % n}, device_id_type=MESH
        )
    stage = pltpu.make_async_copy(
        cash_flows.at[:, :, pl.ds(pl.multiple_of(me * own, own), own)], stage_ref, own_sem.at[0]
    )
    stage.start()
    pl.semaphore_wait(barrier, n - 1)

    stride = n // 2 - 1
    hops = [(i * stride) % n for i in range(1, n)]

    def flow_copy(slot, sender, receiver, device):
        leg = slot // (n - 1)
        return remote(
            cash_flows.at[leg, :, pl.ds(pl.multiple_of(receiver * own, own), own)],
            flows_out.at[pl.ds(pl.multiple_of(sender * rows, rows), rows), pl.ds(leg * own, own)],
            flow_send.at[slot],
            flow_recv.at[slot],
            device,
        )

    def flow_out(slot):
        to = (me + hops[slot % (n - 1)]) % n
        return flow_copy(slot, me, to, to)

    def flow_in(slot):
        source = (me + n - hops[slot % (n - 1)]) % n
        return flow_copy(slot, source, me, source)

    count = (n - 1) * legs
    fills = depth + 3
    started = [0]

    def fill(upto):
        for slot in range(started[0], min(count, upto)):
            flow_out(slot).start()
        started[0] = max(started[0], min(count, upto))

    share = -(-count // fills)
    fill(share)

    chunk = math.gcd(width, 512)
    unit = jnp.ones((1, chunk), jnp.float32)
    zero = jnp.zeros((1, chunk), jnp.float32)
    last = []
    for c in range(width // chunk):
        lanes = pl.ds(c * chunk, chunk)
        pull = reversion[lanes].reshape(1, chunk) * month_step
        sway = volatility[lanes].reshape(1, chunk) * root_step
        persist = 1.0 - pull

        def month(t, carry):
            rate, power, reach, total = carry
            shock = shocks[pl.ds(t, 1), lanes]
            rate = persist * rate + (pull * long_mean[t] + sway * shock)
            power = persist * power
            reach = reach + power
            total = total + (rate + price_scale * shock + price_drift)
            reach_ref[pl.ds(t, 1), lanes] = reach
            total_ref[pl.ds(t, 1), lanes] = total
            return rate, power, reach, total

        rate, power, reach, total = lax.fori_loop(
            0, rows, month, (zero, unit, zero, zero), unroll=4
        )
        part_ref[spot, 0:1, lanes] = rate
        part_ref[spot, 1:2, lanes] = total
        last.append((power, reach))
    power = jnp.concatenate([one[0] for one in last], axis=1)
    reach = jnp.concatenate([one[1] for one in last], axis=1)

    def part_copy(k, slot, device):
        return remote(
            part_ref.at[slot], part_ref.at[slot], part_send.at[k], part_recv.at[k], device
        )

    for k in range(1, team):
        part_copy(k, spot, z * team + (spot + k) % team).start()
    fill(2 * share)
    for k in range(1, team):
        source = (spot + team - k) % team
        part_copy(k, source, z * team + source).wait_recv()

    rate, total = part_ref[0, 0:1], part_ref[0, 1:2]
    level_power, level_reach = power, reach
    for j in range(1, team):
        rate, total = (
            power * rate + part_ref[j, 0:1],
            total + reach * rate + part_ref[j, 1:2],
        )
        level_reach = level_reach + reach * level_power
        level_power = power * level_power
    level_ref[z, 0:1] = rate
    level_ref[z, 1:2] = total

    def level_copy(k, slot, device):
        return remote(
            level_ref.at[slot], level_ref.at[slot], level_send.at[k], level_recv.at[k], device
        )

    for k in range(1, depth):

        @pl.when(z + k < depth)
        def _():
            level_copy(k, z, place(z + k, side, core)).start()

    fill(3 * share)

    for k in range(1, depth):

        @pl.when(z - k >= 0)
        def _():
            level_copy(k, z - k, place(z - k, side, core)).wait_recv()

    def past_level(j, state):
        rate, total = state
        return (
            level_power * rate + level_ref[j, 0:1],
            total + level_reach * rate + level_ref[j, 1:2],
        )

    def past_part(j, state):
        rate, total = state
        return power * rate + part_ref[j, 0:1], total + reach * rate + part_ref[j, 1:2]

    state = (start_rate[...].reshape(1, width), jnp.zeros((1, width), jnp.float32))
    state = lax.fori_loop(0, z, past_level, state)
    rate, total = lax.fori_loop(0, spot, past_part, state)
    exponent = total + reach_ref[...] * rate + total_ref[...]
    block_ref[...] = jnp.exp(-month_step * exponent).astype(jnp.bfloat16)

    def months(m):
        return discount_out.at[pl.ds(pl.multiple_of(m * rows, rows), rows)]

    waits = []

    def send(cond, make):
        waits.append((cond, make))
        if cond is None:
            make().start()
        else:
            pl.when(cond)(lambda: make().start())

    def up_copy(h, shard, src, device):
        return remote(src, months(shard), up_send.at[h], up_recv.at[h], device)

    def down_copy(h, shard, src, device):
        return remote(src, months(shard), down_send.at[h], down_recv.at[h], device)

    def side_copy(level, shard, src, device):
        return remote(src, months(shard), side_send.at[level], side_recv.at[level], device)

    def twin_copy(level, lane, shard, src, device):
        slot = level * sides + lane
        return remote(src, months(shard), twin_send.at[slot], twin_recv.at[slot], device)

    def beside(cond, level, src):
        shard = place(level, side, core)
        if sides > 1:
            send(cond, lambda: side_copy(level, shard, src, place(z, 1 - side, core)))
        send(cond, lambda: twin_copy(level, side, shard, src, place(z, side, 1 - core)))

    def across(cond, level):
        shard = place(level, 1 - side, core)

        def take():
            side_copy(level, shard, months(shard), place(z, 1 - side, core)).wait_recv()

        if cond is None:
            take()
        else:
            pl.when(cond)(take)
        send(
            cond,
            lambda: twin_copy(
                level, 1 - side, shard, months(shard), place(z, side, 1 - core)
            ),
        )

    keep = pltpu.make_async_copy(block_ref, months(me), own_sem.at[1])
    keep.start()
    send(z + 1 < depth, lambda: up_copy(0, me, block_ref, place(z + 1, side, core)))
    send(z > 0, lambda: down_copy(0, me, block_ref, place(z - 1, side, core)))
    beside(None, z, block_ref)
    fill(4 * share)
    for h in range(1, depth):
        low, high = place(z - h, side, core), place(z + h, side, core)

        @pl.when(z - h >= 0)
        def _():
            up_copy(h - 1, low, months(low), place(z - 1, side, core)).wait_recv()

        send(
            (z - h >= 0) & (z + 1 < depth),
            lambda h=h, low=low: up_copy(h, low, months(low), place(z + 1, side, core)),
        )

        @pl.when(z + h < depth)
        def _():
            down_copy(h - 1, high, months(high), place(z + 1, side, core)).wait_recv()

        send(
            (z + h < depth) & (z > 0),
            lambda h=h, high=high: down_copy(h, high, months(high), place(z - 1, side, core)),
        )
        beside(z - h >= 0, z - h, months(low))
        beside(z + h < depth, z + h, months(high))
        if sides > 1:
            if h == 1:
                across(None, z)
            else:
                across(z - h + 1 >= 0, z - h + 1)
                across(z + h - 1 < depth, z + h - 1)
        fill((4 + h) * share)
    if sides > 1:
        if depth == 1:
            across(None, z)
        else:
            across(z - depth + 1 >= 0, z - depth + 1)
            across(z + depth - 1 < depth, z + depth - 1)
    fill(count)

    stage.wait()
    for leg in range(legs):
        pltpu.make_async_copy(
            stage_ref.at[leg],
            flows_out.at[pl.ds(pl.multiple_of(me * rows, rows), rows), pl.ds(leg * own, own)],
            own_sem.at[2 + leg],
        ).start()
    for level in range(depth):
        for lane in range(sides):
            shard = place(level, lane, 1 - core)
            twin_copy(level, lane, shard, months(shard), place(z, side, 1 - core)).wait_recv()
    for slot in range(count):
        flow_in(slot).wait_recv()
    for leg in range(legs):
        pltpu.make_async_copy(
            stage_ref.at[leg],
            flows_out.at[pl.ds(pl.multiple_of(me * rows, rows), rows), pl.ds(leg * own, own)],
            own_sem.at[2 + leg],
        ).wait()
    keep.wait()
    for k in range(1, team):
        part_copy(k, spot, z * team + (spot + k) % team).wait_send()
    for k in range(1, depth):

        @pl.when(z + k < depth)
        def _():
            level_copy(k, z, place(z + k, side, core)).wait_send()

    for cond, make in waits:
        if cond is None:
            make().wait_send()
        else:
            pl.when(cond)(lambda make=make: make().wait_send())
    for slot in range(count):
        flow_out(slot).wait_send()


def local(n, sides, shocks, long_mean, reversion, volatility, start_rate, cash_flows):
    rows, width = shocks.shape
    legs, _, cells = cash_flows.shape
    own = cells // n
    team = sides * CORES
    depth = n // team
    count = (n - 1) * legs
    dma = pltpu.SemaphoreType.DMA
    vmem = pl.BlockSpec(memory_space=pltpu.VMEM)
    anywhere = pl.BlockSpec(memory_space=pl.ANY)
    flows, discount = pl.pallas_call(
        functools.partial(kernel, n, sides),
        out_shape=(
            jax.ShapeDtypeStruct((n * rows, legs * own), jnp.bfloat16),
            jax.ShapeDtypeStruct((n * rows, width), jnp.bfloat16),
        ),
        in_specs=[vmem, pl.BlockSpec(memory_space=pltpu.SMEM), vmem, vmem, vmem, anywhere],
        out_specs=(anywhere, anywhere),
        scratch_shapes=[
            pltpu.VMEM((rows, width), jnp.float32),
            pltpu.VMEM((rows, width), jnp.float32),
            pltpu.VMEM((team, 2, width), jnp.float32),
            pltpu.VMEM((depth, 2, width), jnp.float32),
            pltpu.VMEM((rows, width), jnp.bfloat16),
            pltpu.VMEM((legs, rows, own), jnp.bfloat16),
            dma((count,)),
            dma((count,)),
            dma((team,)),
            dma((team,)),
            dma((depth,)),
            dma((depth,)),
            dma((depth,)),
            dma((depth,)),
            dma((depth,)),
            dma((depth,)),
            dma((depth,)),
            dma((depth,)),
            dma((n // CORES,)),
            dma((n // CORES,)),
            dma((2 + legs,)),
        ],
        compiler_params=pltpu.CompilerParams(collective_id=0, has_side_effects=True),
        name="exchange",
    )(shocks, long_mean, reversion, volatility, start_rate, cash_flows)
    value = lax.dot_general(
        flows, discount, (((0,), (0,)), ((), ())), preferred_element_type=jnp.float32
    )
    return value.astype(jnp.bfloat16).reshape(legs, own, width)


def solution(mesh):
    n = mesh.shape["month"]
    sides = max(1, 4 // mesh.shape["groups"])
    placed = (
        P("month", "groups"),
        P("month"),
        P("groups"),
        P("groups"),
        P("groups"),
        P(None, "month", "groups"),
    )
    return jax.shard_map(
        functools.partial(local, n, sides),
        mesh=mesh,
        in_specs=placed,
        out_specs=P(None, ("groups", "month"), None),
        check_vma=False,
    )
```

```python
import functools
import math

import jax
import jax.numpy as jnp
from jax import lax
from jax.experimental import pallas as pl
from jax.experimental.pallas import tpu as pltpu
from jax.sharding import PartitionSpec as P

month_step = 1.0 / 12.0
root_step = math.sqrt(1.0 / 12.0)
risk_price = 0.15
price_scale = risk_price * math.sqrt(12.0)
price_drift = 0.5 * risk_price * risk_price
MESH = pl.DeviceIdType.MESH
CORES = 2
VMEM_BYTES = 67_043_328
SLACK = 65536


def product(flows, discount, first, cells, out, row, after=None):
    width = discount.shape[1]
    tall, wide = math.gcd(cells, 256), math.gcd(width, 1024)
    for tile in range(cells // tall):
        for c in range(width // wide):
            cols = pl.ds(c * wide, wide)
            value = lax.dot_general(
                flows[:, pl.ds(first + tile * tall, tall)],
                discount[:, cols],
                (((0,), (0,)), ((), ())),
                preferred_element_type=jnp.float32,
            )
            out[pl.ds(row + tile * tall, tall), cols] = value.astype(jnp.bfloat16)
        if after is not None:
            after(tile, tall)


def finish(flows, discount, done, out, last, sems):
    cells = last.shape[0]
    ready, width = done.shape
    parts = ready // cells

    def ship(k):
        rows = pl.ds(k * cells, cells)
        return pltpu.make_async_copy(done.at[rows], out.at[rows], sems.at[k])

    def tail(tile, tall):
        return pltpu.make_async_copy(
            last.at[pl.ds(tile * tall, tall)],
            out.at[pl.ds(ready + tile * tall, tall)],
            sems.at[parts + tile],
        )

    for k in range(parts):
        ship(k).start()
    product(flows, discount, ready, cells, last, 0, lambda tile, tall: tail(tile, tall).start())
    for k in range(parts):
        ship(k).wait()
    tall = math.gcd(cells, 256)
    for tile in range(cells // tall):
        tail(tile, tall).wait()


def kernel(
    n,
    sides,
    shocks,
    long_mean,
    reversion,
    volatility,
    start_rate,
    cash_flows,
    flows_out,
    discount_out,
    done_out,
    reach_ref,
    total_ref,
    part_ref,
    level_ref,
    flow_send,
    flow_recv,
    part_send,
    part_recv,
    level_send,
    level_recv,
    up_send,
    up_recv,
    down_send,
    down_recv,
    side_send,
    side_recv,
    twin_send,
    twin_recv,
    own_sem,
):
    rows, width = shocks.shape
    legs = cash_flows.shape[0]
    own = cash_flows.shape[2] // n
    team = sides * CORES
    depth = n // team
    me = lax.axis_index("month")
    z, spot = me // team, me % team
    side, core = spot // CORES, spot % CORES
    place = lambda z, side, core: (z * sides + side) * CORES + core

    def remote(src, dst, send, recv, device):
        return pltpu.make_async_remote_copy(
            src_ref=src,
            dst_ref=dst,
            send_sem=send,
            recv_sem=recv,
            device_id={"month": device},
            device_id_type=MESH,
        )

    barrier = pltpu.get_barrier_semaphore()
    for k in range(1, n):
        pl.semaphore_signal(
            barrier, inc=1, device_id={"month": (me + k) % n}, device_id_type=MESH
        )
    def keep(leg):
        return pltpu.make_async_copy(
            cash_flows.at[leg, :, pl.ds(pl.multiple_of(me * own, own), own)],
            flows_out.at[pl.ds(pl.multiple_of(me * rows, rows), rows), pl.ds(leg * own, own)],
            own_sem.at[leg],
        )

    for leg in range(legs):
        keep(leg).start()
    pl.semaphore_wait(barrier, n - 1)

    stride = n // 2 - 1
    hops = [(i * stride) % n for i in range(1, n)]

    def flow_copy(slot, sender, receiver, device):
        leg = slot // (n - 1)
        return remote(
            cash_flows.at[leg, :, pl.ds(pl.multiple_of(receiver * own, own), own)],
            flows_out.at[pl.ds(pl.multiple_of(sender * rows, rows), rows), pl.ds(leg * own, own)],
            flow_send.at[slot],
            flow_recv.at[slot],
            device,
        )

    def flow_out(slot):
        to = (me + hops[slot % (n - 1)]) % n
        return flow_copy(slot, me, to, to)

    def flow_in(slot):
        source = (me + n - hops[slot % (n - 1)]) % n
        return flow_copy(slot, source, me, source)

    count = (n - 1) * legs
    fills = depth + 8
    started = [0]

    def fill(upto):
        for slot in range(started[0], min(count, upto)):
            flow_out(slot).start()
        started[0] = max(started[0], min(count, upto))

    share = -(-count // fills)
    fill(share)

    chunk = math.gcd(width, 512)
    unit = jnp.ones((1, chunk), jnp.float32)
    zero = jnp.zeros((1, chunk), jnp.float32)
    last = []
    for c in range(width // chunk):
        lanes = pl.ds(c * chunk, chunk)
        pull = reversion[lanes].reshape(1, chunk) * month_step
        sway = volatility[lanes].reshape(1, chunk) * root_step
        persist = 1.0 - pull

        def month(t, carry):
            rate, power, reach, total = carry
            shock = shocks[pl.ds(t, 1), lanes]
            rate = persist * rate + (pull * long_mean[t] + sway * shock)
            power = persist * power
            reach = reach + power
            total = total + (rate + price_scale * shock + price_drift)
            reach_ref[pl.ds(t, 1), lanes] = reach
            total_ref[pl.ds(t, 1), lanes] = total
            return rate, power, reach, total

        rate, power, reach, total = lax.fori_loop(
            0, rows, month, (zero, unit, zero, zero), unroll=4
        )
        part_ref[spot, 0:1, lanes] = rate
        part_ref[spot, 1:2, lanes] = total
        last.append((power, reach))
    power = jnp.concatenate([one[0] for one in last], axis=1)
    reach = jnp.concatenate([one[1] for one in last], axis=1)

    def part_copy(k, slot, device):
        return remote(
            part_ref.at[slot], part_ref.at[slot], part_send.at[k], part_recv.at[k], device
        )

    for k in range(1, team):
        part_copy(k, spot, z * team + (spot + k) % team).start()
    fill(2 * share)
    for k in range(1, team):
        source = (spot + team - k) % team
        part_copy(k, source, z * team + source).wait_recv()

    rate, total = part_ref[0, 0:1], part_ref[0, 1:2]
    level_power, level_reach = power, reach
    for j in range(1, team):
        rate, total = (
            power * rate + part_ref[j, 0:1],
            total + reach * rate + part_ref[j, 1:2],
        )
        level_reach = level_reach + reach * level_power
        level_power = power * level_power
    level_ref[z, 0:1] = rate
    level_ref[z, 1:2] = total

    def level_copy(k, slot, device):
        return remote(
            level_ref.at[slot], level_ref.at[slot], level_send.at[k], level_recv.at[k], device
        )

    for k in range(1, depth):

        @pl.when(z + k < depth)
        def _():
            level_copy(k, z, place(z + k, side, core)).start()

    fill(3 * share)

    for k in range(1, depth):

        @pl.when(z - k >= 0)
        def _():
            level_copy(k, z - k, place(z - k, side, core)).wait_recv()

    def past_level(j, state):
        rate, total = state
        return (
            level_power * rate + level_ref[j, 0:1],
            total + level_reach * rate + level_ref[j, 1:2],
        )

    def past_part(j, state):
        rate, total = state
        return power * rate + part_ref[j, 0:1], total + reach * rate + part_ref[j, 1:2]

    state = (start_rate[...].reshape(1, width), jnp.zeros((1, width), jnp.float32))
    state = lax.fori_loop(0, z, past_level, state)
    rate, total = lax.fori_loop(0, spot, past_part, state)
    exponent = total + reach_ref[...] * rate + total_ref[...]
    discount_out[pl.ds(pl.multiple_of(me * rows, rows), rows), :] = jnp.exp(
        -month_step * exponent
    ).astype(jnp.bfloat16)

    def months(m):
        return discount_out.at[pl.ds(pl.multiple_of(m * rows, rows), rows)]

    waits = []

    def send(cond, make):
        waits.append((cond, make))
        if cond is None:
            make().start()
        else:
            pl.when(cond)(lambda: make().start())

    def up_copy(h, shard, src, device):
        return remote(src, months(shard), up_send.at[h], up_recv.at[h], device)

    def down_copy(h, shard, src, device):
        return remote(src, months(shard), down_send.at[h], down_recv.at[h], device)

    def side_copy(level, shard, src, device):
        return remote(src, months(shard), side_send.at[level], side_recv.at[level], device)

    def twin_copy(level, lane, shard, src, device):
        slot = level * sides + lane
        return remote(src, months(shard), twin_send.at[slot], twin_recv.at[slot], device)

    def beside(cond, level, src):
        shard = place(level, side, core)
        if sides > 1:
            send(cond, lambda: side_copy(level, shard, src, place(z, 1 - side, core)))
        send(cond, lambda: twin_copy(level, side, shard, src, place(z, side, 1 - core)))

    def across(cond, level):
        shard = place(level, 1 - side, core)

        def take():
            side_copy(level, shard, months(shard), place(z, 1 - side, core)).wait_recv()

        if cond is None:
            take()
        else:
            pl.when(cond)(take)
        send(
            cond,
            lambda: twin_copy(
                level, 1 - side, shard, months(shard), place(z, side, 1 - core)
            ),
        )

    send(z + 1 < depth, lambda: up_copy(0, me, months(me), place(z + 1, side, core)))
    send(z > 0, lambda: down_copy(0, me, months(me), place(z - 1, side, core)))
    beside(None, z, months(me))
    fill(4 * share)
    for h in range(1, depth):
        low, high = place(z - h, side, core), place(z + h, side, core)

        @pl.when(z - h >= 0)
        def _():
            up_copy(h - 1, low, months(low), place(z - 1, side, core)).wait_recv()

        send(
            (z - h >= 0) & (z + 1 < depth),
            lambda h=h, low=low: up_copy(h, low, months(low), place(z + 1, side, core)),
        )

        @pl.when(z + h < depth)
        def _():
            down_copy(h - 1, high, months(high), place(z + 1, side, core)).wait_recv()

        send(
            (z + h < depth) & (z > 0),
            lambda h=h, high=high: down_copy(h, high, months(high), place(z - 1, side, core)),
        )
        beside(z - h >= 0, z - h, months(low))
        beside(z + h < depth, z + h, months(high))
        if sides > 1:
            if h == 1:
                across(None, z)
            else:
                across(z - h + 1 >= 0, z - h + 1)
                across(z + h - 1 < depth, z + h - 1)
        fill((4 + h) * share)
    if sides > 1:
        if depth == 1:
            across(None, z)
        else:
            across(z - depth + 1 >= 0, z - depth + 1)
            across(z + depth - 1 < depth, z + depth - 1)
    fill(count)

    for level in range(depth):
        for lane in range(sides):
            shard = place(level, lane, 1 - core)
            twin_copy(level, lane, shard, months(shard), place(z, side, 1 - core)).wait_recv()
    for leg in range(legs):
        for slot in range(leg * (n - 1), (leg + 1) * (n - 1)):
            flow_in(slot).wait_recv()
        keep(leg).wait()
        if leg < legs - 1:
            product(flows_out, discount_out, leg * own, own, done_out, leg * own)
    for k in range(1, team):
        part_copy(k, spot, z * team + (spot + k) % team).wait_send()
    for k in range(1, depth):

        @pl.when(z + k < depth)
        def _():
            level_copy(k, z, place(z + k, side, core)).wait_send()

    for cond, make in waits:
        if cond is None:
            make().wait_send()
        else:
            pl.when(cond)(lambda make=make: make().wait_send())
    for slot in range(count):
        flow_out(slot).wait_send()


def local(n, sides, shocks, long_mean, reversion, volatility, start_rate, cash_flows):
    rows, width = shocks.shape
    legs, _, cells = cash_flows.shape
    own = cells // n
    team = sides * CORES
    depth = n // team
    count = (n - 1) * legs
    held = 2 * (n * rows * (legs * own + width) + (legs - 1) * own * width) + SLACK
    dma = pltpu.SemaphoreType.DMA
    vmem = pl.BlockSpec(memory_space=pltpu.VMEM)
    anywhere = pl.BlockSpec(memory_space=pltpu.HBM)
    flows, discount, done = pl.pallas_call(
        functools.partial(kernel, n, sides),
        out_shape=(
            pltpu.VMEM((n * rows, legs * own), jnp.bfloat16),
            pltpu.VMEM((n * rows, width), jnp.bfloat16),
            pltpu.VMEM(((legs - 1) * own, width), jnp.bfloat16),
        ),
        in_specs=[vmem, pl.BlockSpec(memory_space=pltpu.SMEM), vmem, vmem, vmem, anywhere],
        out_specs=(vmem, vmem, vmem),
        scratch_shapes=[
            pltpu.VMEM((rows, width), jnp.float32),
            pltpu.VMEM((rows, width), jnp.float32),
            pltpu.VMEM((team, 2, width), jnp.float32),
            pltpu.VMEM((depth, 2, width), jnp.float32),
            dma((count,)),
            dma((count,)),
            dma((team,)),
            dma((team,)),
            dma((depth,)),
            dma((depth,)),
            dma((depth,)),
            dma((depth,)),
            dma((depth,)),
            dma((depth,)),
            dma((depth,)),
            dma((depth,)),
            dma((n // CORES,)),
            dma((n // CORES,)),
            dma((legs,)),
        ],
        compiler_params=pltpu.CompilerParams(
            collective_id=0, has_side_effects=True, vmem_limit_bytes=VMEM_BYTES - held
        ),
        name="exchange",
    )(shocks, long_mean, reversion, volatility, start_rate, cash_flows)
    tiles = own // math.gcd(own, 256)
    present = pl.pallas_call(
        finish,
        out_shape=jax.ShapeDtypeStruct((legs * own, width), jnp.bfloat16),
        in_specs=[vmem, vmem, vmem],
        out_specs=anywhere,
        scratch_shapes=[
            pltpu.VMEM((own, width), jnp.bfloat16),
            dma((legs - 1 + tiles,)),
        ],
        compiler_params=pltpu.CompilerParams(vmem_limit_bytes=16 << 20),
        name="finish",
    )(flows, discount, done)
    return present.reshape(legs, own, width)


def solution(mesh):
    n = mesh.shape["month"]
    sides = max(1, 4 // mesh.shape["groups"])
    placed = (
        P("month", "groups"),
        P("month"),
        P("groups"),
        P("groups"),
        P("groups"),
        P(None, "month", "groups"),
    )
    return jax.shard_map(
        functools.partial(local, n, sides),
        mesh=mesh,
        in_specs=placed,
        out_specs=P(None, ("groups", "month"), None),
        check_vma=False,
    )
```

```python
import functools
import math

import jax
import jax.numpy as jnp
from jax import lax
from jax.experimental import pallas as pl
from jax.experimental.pallas import tpu as pltpu
from jax.sharding import PartitionSpec as P

month_step = 1.0 / 12.0
root_step = math.sqrt(1.0 / 12.0)
risk_price = 0.15
price_scale = risk_price * math.sqrt(12.0)
price_drift = 0.5 * risk_price * risk_price
MESH = pl.DeviceIdType.MESH
CORES = 2
VMEM_BYTES = 67_043_328
SLACK = 65536


def product(flows, discount, first, cells, out, row, after=None):
    width = discount.shape[1]
    tall, wide = math.gcd(cells, 256), math.gcd(width, 1024)
    for tile in range(cells // tall):
        for c in range(width // wide):
            cols = pl.ds(c * wide, wide)
            value = lax.dot_general(
                flows[:, pl.ds(first + tile * tall, tall)],
                discount[:, cols],
                (((0,), (0,)), ((), ())),
                preferred_element_type=jnp.float32,
            )
            out[pl.ds(row + tile * tall, tall), cols] = value.astype(jnp.bfloat16)
        if after is not None:
            after(tile, tall)


def finish(flows, discount, done, out, last, sems):
    cells = last.shape[0]
    ready, width = done.shape
    parts = ready // cells

    def ship(k):
        rows = pl.ds(k * cells, cells)
        return pltpu.make_async_copy(done.at[rows], out.at[rows], sems.at[k])

    def tail(tile, tall):
        return pltpu.make_async_copy(
            last.at[pl.ds(tile * tall, tall)],
            out.at[pl.ds(ready + tile * tall, tall)],
            sems.at[parts + tile],
        )

    for k in range(parts):
        ship(k).start()
    product(flows, discount, ready, cells, last, 0, lambda tile, tall: tail(tile, tall).start())
    for k in range(parts):
        ship(k).wait()
    tall = math.gcd(cells, 256)
    for tile in range(cells // tall):
        tail(tile, tall).wait()


def kernel(
    n,
    sides,
    shocks,
    long_mean,
    reversion,
    volatility,
    start_rate,
    cash_flows,
    flows_out,
    discount_out,
    done_out,
    reach_ref,
    total_ref,
    part_ref,
    level_ref,
    flow_send,
    flow_recv,
    part_send,
    part_recv,
    level_send,
    level_recv,
    up_send,
    up_recv,
    down_send,
    down_recv,
    side_send,
    side_recv,
    twin_send,
    twin_recv,
    own_sem,
):
    rows, width = shocks.shape
    legs = cash_flows.shape[0]
    own = cash_flows.shape[2] // n
    team = sides * CORES
    depth = n // team
    me = lax.axis_index("month")
    z, spot = me // team, me % team
    side, core = spot // CORES, spot % CORES
    place = lambda z, side, core: (z * sides + side) * CORES + core

    def remote(src, dst, send, recv, device):
        return pltpu.make_async_remote_copy(
            src_ref=src,
            dst_ref=dst,
            send_sem=send,
            recv_sem=recv,
            device_id={"month": device},
            device_id_type=MESH,
        )

    barrier = pltpu.get_barrier_semaphore()
    for k in range(1, n):
        pl.semaphore_signal(
            barrier, inc=1, device_id={"month": (me + k) % n}, device_id_type=MESH
        )
    def keep(leg):
        return pltpu.make_async_copy(
            cash_flows.at[leg, :, pl.ds(pl.multiple_of(me * own, own), own)],
            flows_out.at[pl.ds(pl.multiple_of(me * rows, rows), rows), pl.ds(leg * own, own)],
            own_sem.at[leg],
        )

    for leg in range(legs):
        keep(leg).start()

    stride = n // 2 - 1
    hops = [(i * stride) % n for i in range(1, n)]

    def flow_copy(slot, sender, receiver, device):
        leg = slot // (n - 1)
        return remote(
            cash_flows.at[leg, :, pl.ds(pl.multiple_of(receiver * own, own), own)],
            flows_out.at[pl.ds(pl.multiple_of(sender * rows, rows), rows), pl.ds(leg * own, own)],
            flow_send.at[slot],
            flow_recv.at[slot],
            device,
        )

    def flow_out(slot):
        to = (me + hops[slot % (n - 1)]) % n
        return flow_copy(slot, me, to, to)

    def flow_in(slot):
        source = (me + n - hops[slot % (n - 1)]) % n
        return flow_copy(slot, source, me, source)

    count = (n - 1) * legs
    fills = depth + 8
    started = [0]

    def fill(upto):
        for slot in range(started[0], min(count, upto)):
            flow_out(slot).start()
        started[0] = max(started[0], min(count, upto))

    share = -(-count // fills)
    lead = 3 * share

    chunk = math.gcd(width, 512)
    unit = jnp.ones((1, chunk), jnp.float32)
    zero = jnp.zeros((1, chunk), jnp.float32)
    last = []
    for c in range(width // chunk):
        lanes = pl.ds(c * chunk, chunk)
        pull = reversion[lanes].reshape(1, chunk) * month_step
        sway = volatility[lanes].reshape(1, chunk) * root_step
        persist = 1.0 - pull

        def month(t, carry):
            rate, power, reach, total = carry
            shock = shocks[pl.ds(t, 1), lanes]
            rate = persist * rate + (pull * long_mean[t] + sway * shock)
            power = persist * power
            reach = reach + power
            total = total + (rate + price_scale * shock + price_drift)
            reach_ref[pl.ds(t, 1), lanes] = reach
            total_ref[pl.ds(t, 1), lanes] = total
            return rate, power, reach, total

        rate, power, reach, total = lax.fori_loop(
            0, rows, month, (zero, unit, zero, zero), unroll=4
        )
        part_ref[spot, 0:1, lanes] = rate
        part_ref[spot, 1:2, lanes] = total
        last.append((power, reach))
    power = jnp.concatenate([one[0] for one in last], axis=1)
    reach = jnp.concatenate([one[1] for one in last], axis=1)

    pl.semaphore_wait(barrier, n - 1)

    def part_copy(k, slot, device):
        return remote(
            part_ref.at[slot], part_ref.at[slot], part_send.at[k], part_recv.at[k], device
        )

    for k in range(1, team):
        part_copy(k, spot, z * team + (spot + k) % team).start()
    fill(2 * share)
    for k in range(1, team):
        source = (spot + team - k) % team
        part_copy(k, source, z * team + source).wait_recv()

    rate, total = part_ref[0, 0:1], part_ref[0, 1:2]
    level_power, level_reach = power, reach
    for j in range(1, team):
        rate, total = (
            power * rate + part_ref[j, 0:1],
            total + reach * rate + part_ref[j, 1:2],
        )
        level_reach = level_reach + reach * level_power
        level_power = power * level_power

    def level_copy(device):
        return remote(
            level_ref.at[1], level_ref.at[0], level_send.at[0], level_recv.at[0], device
        )

    fill(lead)

    @pl.when(z == 0)
    def _():
        level_ref[0, 0:1] = start_rate[...].reshape(1, width)
        level_ref[0, 1:2] = jnp.zeros((1, width), jnp.float32)

    @pl.when(z > 0)
    def _():
        level_copy(place(z - 1, side, core)).wait_recv()

    first_rate, first_total = level_ref[0, 0:1], level_ref[0, 1:2]

    @pl.when(z + 1 < depth)
    def _():
        level_ref[1, 0:1] = level_power * first_rate + rate
        level_ref[1, 1:2] = first_total + level_reach * first_rate + total
        level_copy(place(z + 1, side, core)).start()

    def past_part(j, state):
        rate, total = state
        return power * rate + part_ref[j, 0:1], total + reach * rate + part_ref[j, 1:2]

    rate, total = lax.fori_loop(0, spot, past_part, (first_rate, first_total))
    exponent = total + reach_ref[...] * rate + total_ref[...]
    discount_out[pl.ds(pl.multiple_of(me * rows, rows), rows), :] = jnp.exp(
        -month_step * exponent
    ).astype(jnp.bfloat16)

    def months(m):
        return discount_out.at[pl.ds(pl.multiple_of(m * rows, rows), rows)]

    waits = []

    def send(cond, make):
        waits.append((cond, make))
        if cond is None:
            make().start()
        else:
            pl.when(cond)(lambda: make().start())

    def up_copy(h, shard, src, device):
        return remote(src, months(shard), up_send.at[h], up_recv.at[h], device)

    def down_copy(h, shard, src, device):
        return remote(src, months(shard), down_send.at[h], down_recv.at[h], device)

    def side_copy(level, shard, src, device):
        return remote(src, months(shard), side_send.at[level], side_recv.at[level], device)

    def twin_copy(level, lane, shard, src, device):
        slot = level * sides + lane
        return remote(src, months(shard), twin_send.at[slot], twin_recv.at[slot], device)

    def beside(cond, level, src):
        shard = place(level, side, core)
        if sides > 1:
            send(cond, lambda: side_copy(level, shard, src, place(z, 1 - side, core)))
        send(cond, lambda: twin_copy(level, side, shard, src, place(z, side, 1 - core)))

    def across(cond, level):
        shard = place(level, 1 - side, core)

        def take():
            side_copy(level, shard, months(shard), place(z, 1 - side, core)).wait_recv()

        if cond is None:
            take()
        else:
            pl.when(cond)(take)
        send(
            cond,
            lambda: twin_copy(
                level, 1 - side, shard, months(shard), place(z, side, 1 - core)
            ),
        )

    send(z + 1 < depth, lambda: up_copy(0, me, months(me), place(z + 1, side, core)))
    send(z > 0, lambda: down_copy(0, me, months(me), place(z - 1, side, core)))
    beside(None, z, months(me))
    fill(lead + share)
    for h in range(1, depth):
        low, high = place(z - h, side, core), place(z + h, side, core)

        @pl.when(z - h >= 0)
        def _():
            up_copy(h - 1, low, months(low), place(z - 1, side, core)).wait_recv()

        send(
            (z - h >= 0) & (z + 1 < depth),
            lambda h=h, low=low: up_copy(h, low, months(low), place(z + 1, side, core)),
        )

        @pl.when(z + h < depth)
        def _():
            down_copy(h - 1, high, months(high), place(z + 1, side, core)).wait_recv()

        send(
            (z + h < depth) & (z > 0),
            lambda h=h, high=high: down_copy(h, high, months(high), place(z - 1, side, core)),
        )
        beside(z - h >= 0, z - h, months(low))
        beside(z + h < depth, z + h, months(high))
        if sides > 1:
            if h == 1:
                across(None, z)
            else:
                across(z - h + 1 >= 0, z - h + 1)
                across(z + h - 1 < depth, z + h - 1)
        fill(lead + (1 + h) * share)
    if sides > 1:
        if depth == 1:
            across(None, z)
        else:
            across(z - depth + 1 >= 0, z - depth + 1)
            across(z + depth - 1 < depth, z + depth - 1)
    fill(count)

    for level in range(depth):
        for lane in range(sides):
            shard = place(level, lane, 1 - core)
            twin_copy(level, lane, shard, months(shard), place(z, side, 1 - core)).wait_recv()
    for leg in range(legs):
        for slot in range(leg * (n - 1), (leg + 1) * (n - 1)):
            flow_in(slot).wait_recv()
        keep(leg).wait()
        if leg < legs - 1:
            product(flows_out, discount_out, leg * own, own, done_out, leg * own)
    for k in range(1, team):
        part_copy(k, spot, z * team + (spot + k) % team).wait_send()
    @pl.when(z + 1 < depth)
    def _():
        level_copy(place(z + 1, side, core)).wait_send()

    for cond, make in waits:
        if cond is None:
            make().wait_send()
        else:
            pl.when(cond)(lambda make=make: make().wait_send())
    for slot in range(count):
        flow_out(slot).wait_send()


def local(n, sides, shocks, long_mean, reversion, volatility, start_rate, cash_flows):
    rows, width = shocks.shape
    legs, _, cells = cash_flows.shape
    own = cells // n
    team = sides * CORES
    depth = n // team
    count = (n - 1) * legs
    held = 2 * (n * rows * (legs * own + width) + (legs - 1) * own * width) + SLACK
    dma = pltpu.SemaphoreType.DMA
    vmem = pl.BlockSpec(memory_space=pltpu.VMEM)
    anywhere = pl.BlockSpec(memory_space=pltpu.HBM)
    flows, discount, done = pl.pallas_call(
        functools.partial(kernel, n, sides),
        out_shape=(
            pltpu.VMEM((n * rows, legs * own), jnp.bfloat16),
            pltpu.VMEM((n * rows, width), jnp.bfloat16),
            pltpu.VMEM(((legs - 1) * own, width), jnp.bfloat16),
        ),
        in_specs=[vmem, pl.BlockSpec(memory_space=pltpu.SMEM), vmem, vmem, vmem, anywhere],
        out_specs=(vmem, vmem, vmem),
        scratch_shapes=[
            pltpu.VMEM((rows, width), jnp.float32),
            pltpu.VMEM((rows, width), jnp.float32),
            pltpu.VMEM((team, 2, width), jnp.float32),
            pltpu.VMEM((2, 2, width), jnp.float32),
            dma((count,)),
            dma((count,)),
            dma((team,)),
            dma((team,)),
            dma((1,)),
            dma((1,)),
            dma((depth,)),
            dma((depth,)),
            dma((depth,)),
            dma((depth,)),
            dma((depth,)),
            dma((depth,)),
            dma((n // CORES,)),
            dma((n // CORES,)),
            dma((legs,)),
        ],
        compiler_params=pltpu.CompilerParams(
            collective_id=0, has_side_effects=True, vmem_limit_bytes=VMEM_BYTES - held
        ),
        name="exchange",
    )(shocks, long_mean, reversion, volatility, start_rate, cash_flows)
    tiles = own // math.gcd(own, 256)
    present = pl.pallas_call(
        finish,
        out_shape=jax.ShapeDtypeStruct((legs * own, width), jnp.bfloat16),
        in_specs=[vmem, vmem, vmem],
        out_specs=anywhere,
        scratch_shapes=[
            pltpu.VMEM((own, width), jnp.bfloat16),
            dma((legs - 1 + tiles,)),
        ],
        compiler_params=pltpu.CompilerParams(vmem_limit_bytes=16 << 20),
        name="finish",
    )(flows, discount, done)
    return present.reshape(legs, own, width)


def solution(mesh):
    n = mesh.shape["month"]
    sides = max(1, 4 // mesh.shape["groups"])
    placed = (
        P("month", "groups"),
        P("month"),
        P("groups"),
        P("groups"),
        P("groups"),
        P(None, "month", "groups"),
    )
    return jax.shard_map(
        functools.partial(local, n, sides),
        mesh=mesh,
        in_specs=placed,
        out_specs=P(None, ("groups", "month"), None),
        check_vma=False,
    )
```
